32 devices in a mesh: phase: 16 (over z, y, x), lat: 2 (over core).
Axes of the slice: x: 2, y: 2, z: 4, core: 2. Of those that a mesh axis runs over, the one named last changes fastest.
Arguments:
- state_now: float32 [3, 64, 1024], P(None, ('lat', 'phase')), may hold values from -4 to 4
- ocean_depth: float32 [64, 1024], P('lat'), may hold values from 0.5 to 1.5
- coriolis: float32 [64], P('lat'), may hold values from -0.4 to 0.4
- phase_times: float32 [16], P('phase'), may hold values from -6 to 6
- phase_weights: float32 [16], P('phase'), may hold values from 0.00625 to 0.25
Outputs:
- state_next: float32 [3, 64, 1024], P(None, ('lat', 'phase'))
- tendency: float32 [3, 64, 1024], P(None, ('lat', 'phase'))
The draws below stay inside these ranges and needn't reach their ends.
All inputs are finite; a program needn't handle non-finite values.
Results may differ from the reference program's by a relative error of at most 0.00002.
Values sent between devices are 32-bit elements; how exact they have to be, the bound alone decides.
A program may use at most 64 MiB of HBM per device.

```python
import math
import jax
import jax.numpy as jnp
from jax import lax

NLON = 1024
DEG = 8
NLAT = 64
SAMPLES = 16


def steps_of(stream_key, dims, split, least, top_value):
    factor_of, own = 1.0, jax.random.fold_in(stream_key, 6)
    for axis_at, parts in split:
        steps = jnp.exp(jax.random.uniform(jax.random.fold_in(own, axis_at), (parts,), jnp.float32, least / len(split), top_value / len(split)))
        factor_of = factor_of * jnp.repeat(steps, dims[axis_at] // parts).reshape([-1 if axis == axis_at else 1 for axis in range(len(dims))])
    return factor_of


def gaussian(stream_key, shape, deviation, most, pieces=(), held_as=jnp.bfloat16):
    level = steps_of(stream_key, shape, pieces, -0.22, 0.18) if pieces else 1.0
    array = jax.random.normal(stream_key, shape, jnp.float32) * deviation * level
    return jnp.minimum(jnp.maximum(array, -most), most).astype(held_as)


def setup_inputs(seed: int = 0) -> dict:
    streams_of = jax.random.split(jax.random.key(seed), 6)
    return {
        "state_now": gaussian(streams_of[0], (3, NLAT, NLON), 1.0, 4.0, ((1, 32),), jnp.float32),
        "ocean_depth": jnp.clip(0.5 + 1.0 * jax.random.uniform(streams_of[1], (NLAT, NLON), jnp.float32) ** steps_of(streams_of[1], (NLAT, NLON), ((0, 2),), -0.2, 0.2), 0.5, 1.5),
        "coriolis": jnp.clip(jax.random.uniform(streams_of[2], (NLAT,), jnp.float32, -0.4, 0.4) * steps_of(streams_of[2], (NLAT,), ((0, 2),), -0.4, 0.0), -0.4, 0.4),
        "phase_times": jnp.clip(jax.random.uniform(streams_of[3], (SAMPLES,), jnp.float32, -6.0, 6.0) * steps_of(streams_of[3], (SAMPLES,), ((0, 16),), -0.4, 0.0), -6.0, 6.0),
        "phase_weights": jnp.clip(jnp.exp(math.log(0.25) - 3.6888794 * jax.random.uniform(streams_of[4], (SAMPLES,), jnp.float32) ** steps_of(streams_of[4], (SAMPLES,), ((0, 16),), -0.2, 0.2)), 0.00625, 0.25),
    }


radius_scale = 2.5
time_step = 0.5
series_terms = 20


def along_lon(values):
    return (jnp.roll(values, -1, axis=-1) - jnp.roll(values, 1, axis=-1)) * 0.5


def along_lat(values):
    return (values[..., 2:, :] - values[..., :-2, :]) * 0.5


def interior(values):
    return values[..., 1:-1, :]


def wave_operator(fields, coefficients):
    height = fields[:, 0]
    eastward = fields[:, 1]
    northward = fields[:, 2]
    depth_field = coefficients[0]
    rotation = coefficients[1]
    out_height = -(along_lon(interior(depth_field * eastward)) + along_lat(depth_field * northward))
    out_east = -along_lon(interior(height)) + interior(rotation * northward)
    out_north = -along_lat(height) - interior(rotation * eastward)
    return jnp.stack([out_height, out_east, out_north], axis=1) / radius_scale


def advection(fields):
    height = fields[:, 0]
    eastward = fields[:, 1]
    northward = fields[:, 2]
    mid_east = interior(eastward)
    mid_north = interior(northward)
    out_height = -(along_lon(interior(height * eastward)) + along_lat(height * northward))
    out_east = -(mid_east * along_lon(mid_east) + mid_north * along_lat(eastward))
    out_north = -(mid_east * along_lon(mid_north) + mid_north * along_lat(northward))
    return jnp.stack([out_height, out_east, out_north], axis=1)


def series_coeffs(sample_time):
    half_time = sample_time * 0.5
    square = half_time * half_time
    result = []
    for degree in range(DEG + 1):
        summed = jnp.zeros_like(sample_time)
        term_sq = jnp.ones_like(sample_time)
        for series in range(series_terms):
            factor = (-1.0) ** series / (math.factorial(series) * math.factorial(series + degree))
            summed = summed + factor * term_sq
            term_sq = term_sq * square
        result.append(summed * half_time ** degree)
    return result


def pad_rows(values):
    return jnp.pad(values, ((0, 0), (0, 0), (1, 1), (0, 0)))


def exponential(fields, coefficients, sample_time):
    series = series_coeffs(sample_time)
    previous = fields
    accumulated = series[0] * fields
    current = wave_operator(pad_rows(fields), coefficients)
    accumulated = accumulated + 2.0 * series[1] * current
    for degree in range(2, DEG + 1):
        advanced = 2.0 * wave_operator(pad_rows(current), coefficients) + previous
        accumulated = accumulated + 2.0 * series[degree] * advanced
        previous = current
        current = advanced
    return accumulated


def averaged(state_now, coefficients, phase_times, phase_weights):
    def one_sample(summed, paired):
        sample_time, weight = paired
        waves = exponential(state_now[None], coefficients, sample_time)
        pulled = advection(pad_rows(waves))
        returned = exponential(pulled, coefficients, -sample_time)
        return summed + weight * returned[0], None

    summed, unused = lax.scan(one_sample, jnp.zeros_like(state_now), (phase_times, phase_weights))
    return summed


def reference(state_now, ocean_depth, coriolis, phase_times, phase_weights):
    stacked = jnp.stack([ocean_depth, jnp.broadcast_to(coriolis[:, None], ocean_depth.shape)])
    coefficients = jnp.pad(stacked, ((0, 0), (1, 1), (0, 0)))
    first = averaged(state_now, coefficients, phase_times, phase_weights)
    middle = state_now + time_step * first
    second = averaged(middle, coefficients, phase_times, phase_weights)
    tendency = 0.5 * (first + second)
    state_next = state_now + time_step * tendency
    return (state_next, tendency)
```

```python
import functools
import math

import jax
import jax.numpy as jnp
from jax import lax
from jax.experimental import pallas as pl
from jax.experimental.pallas import tpu as pltpu
from jax.sharding import PartitionSpec as P

DEG = 8
HALO = 2 * DEG + 1
BLOCK = 8
LANES = 128
SUBLANES = 8

radius_scale = 2.5
time_step = 0.5
series_terms = 20

HEIGHT_SCALE = 1.0 / radius_scale
DEPTH_SCALE = 1.0 / (radius_scale * radius_scale)
ROTATION_SCALE = 2.0 / radius_scale


def kernel(
    phases,
    lats,
    state,
    depth,
    coriolis,
    times,
    weights,
    next_out,
    tend_out,
    own,
    gathered,
    window,
    coef_field,
    even,
    odd,
    waves,
    pulled,
    partial,
    parts,
    first,
    series,
    gather_send,
    gather_recv,
    sum_send,
    sum_recv,
    halo_send,
    halo_recv,
):
    rows, share = depth.shape[0], state.shape[1]
    me, lat = lax.axis_index("phase"), lax.axis_index("lat")
    below = (lat + lats - 1) // lats
    above = (2 * lats - 2 - lat) // lats
    span = window.shape[2]

    zero = jnp.zeros((HALO, SUBLANES, LANES), jnp.float32)
    for array in (window.at[0], window.at[1]):
        for field in range(3):
            array[field, 0:HALO] = zero
            array[field, HALO + rows : span] = zero
    for field in range(2):
        coef_field[field, 0:HALO] = zero
        coef_field[field, HALO + rows : span] = zero

    barrier = pltpu.get_barrier_semaphore()

    def greet(step, carry):
        peer = lax.rem(me + step, phases)
        pl.semaphore_signal(barrier, inc=1, device_id={"phase": peer})
        return carry

    lax.fori_loop(1, phases, greet, 0)

    @pl.when(lat > 0)
    def _():
        pl.semaphore_signal(barrier, inc=1, device_id={"lat": lat - 1})

    @pl.when(lat < lats - 1)
    def _():
        pl.semaphore_signal(barrier, inc=1, device_id={"lat": lat + 1})

    for s in range(SUBLANES):
        lanes = pl.ds(s * LANES, LANES)
        for field in range(3):
            piece = state[field, :, lanes]
            own[field, :, s, :] = piece * HEIGHT_SCALE if field == 0 else piece
        coef_field[0, HALO : HALO + rows, s, :] = depth[:, lanes] * DEPTH_SCALE
    for row in range(rows):
        coef_field[1, HALO + row] = jnp.full((SUBLANES, LANES), coriolis[row] * ROTATION_SCALE, jnp.float32)
    gathered[0, :, pl.ds(me * share, share)] = own[...]

    half_time = jnp.full((SUBLANES, LANES), times[0] * 0.5, jnp.float32)
    weight = jnp.full((SUBLANES, LANES), weights[0], jnp.float32)
    square = half_time * half_time
    power = jnp.ones_like(half_time)
    for degree in range(DEG + 1):
        summed = jnp.zeros_like(square)
        for term in reversed(range(series_terms)):
            factor = (-1.0) ** term / (math.factorial(term) * math.factorial(term + degree))
            summed = summed * square + factor
        value = summed * power
        if degree > 0:
            value = 2.0 * value
        series[0, degree] = value
        series[1, degree] = weight * (value if degree % 2 == 0 else -value)
        power = power * half_time

    zero = jnp.zeros((span, SUBLANES, LANES), jnp.float32)
    for field in range(3):
        waves[field] = zero
        pulled[field] = zero

    pl.semaphore_wait(barrier, phases - 1 + below + above)

    def gather_copy(which, step, sending):
        peer = lax.rem(me + step, phases)
        at = pl.ds(me * share, share)
        return pltpu.make_async_remote_copy(
            src_ref=gathered.at[which, :, at],
            dst_ref=gathered.at[which, :, at],
            send_sem=gather_send.at[which, step],
            recv_sem=gather_recv.at[which, step],
            device_id={"phase": peer},
        )

    def sum_copy(which, step):
        peer = lax.rem(me + step, phases)
        return pltpu.make_async_remote_copy(
            src_ref=partial.at[which, :, pl.ds(peer * share, share)],
            dst_ref=parts.at[which, step],
            send_sem=sum_send.at[which, step],
            recv_sem=sum_recv.at[which, step],
            device_id={"phase": peer},
        )

    def each_peer(fn):
        def body(step, carry):
            fn(step)
            return carry

        lax.fori_loop(1, phases, body, 0)

    def edge_copies(array, index):
        up = pltpu.make_async_remote_copy(
            src_ref=array.at[:, pl.ds(rows, HALO)],
            dst_ref=array.at[:, pl.ds(0, HALO)],
            send_sem=halo_send.at[index, 0],
            recv_sem=halo_recv.at[index, 0],
            device_id={"lat": lat + 1},
        )
        down = pltpu.make_async_remote_copy(
            src_ref=array.at[:, pl.ds(HALO, HALO)],
            dst_ref=array.at[:, pl.ds(HALO + rows, HALO)],
            send_sem=halo_send.at[index, 1],
            recv_sem=halo_recv.at[index, 1],
            device_id={"lat": lat - 1},
        )
        return up, down

    def edges_start(array, index):
        up, down = edge_copies(array, index)
        pl.when(lat < lats - 1)(up.start)
        pl.when(lat > 0)(down.start)

    def edges_wait(array, index):
        up, down = edge_copies(array, index)

        @pl.when(lat < lats - 1)
        def _():
            up.wait_send()
            down.wait_recv()

        @pl.when(lat > 0)
        def _():
            down.wait_send()
            up.wait_recv()

    lane = lax.broadcasted_iota(jnp.int32, (BLOCK, SUBLANES, LANES), 2)
    last_lane, first_lane = lane == LANES - 1, lane == 0

    def lon_diff(values):
        after = pltpu.roll(values, LANES - 1, 2)
        after = jnp.where(last_lane, pltpu.roll(after, SUBLANES - 1, 1), after)
        before = pltpu.roll(values, 1, 2)
        before = jnp.where(first_lane, pltpu.roll(before, 1, 1), before)
        return after - before

    def for_blocks(margin, fn):
        start = HALO - margin * below

        def body(i, carry):
            fn(start + i * BLOCK)
            return carry

        if lats == 2:
            lax.fori_loop(0, (rows + margin) // BLOCK, body, 0, unroll=True)
        else:
            lax.fori_loop(0, (rows + margin * (below + above)) // BLOCK, body, 0)

    def twice_operator(source, at):
        mid, wide = pl.ds(at, BLOCK), pl.ds(at - 1, BLOCK + 2)
        height = source[0, wide]
        east = source[1, mid]
        north = source[2, wide]
        flux = coef_field[0, wide] * north
        rotation = coef_field[1, mid]
        height_part = lon_diff(coef_field[0, mid] * east) + (flux[2:] - flux[:-2])
        east_part = lon_diff(height[1:-1]) - rotation * north[1:-1]
        north_part = (height[2:] - height[:-2]) + rotation * east
        return height_part, east_part, north_part

    def clenshaw(target, source, base, factor, margin):
        def body(at):
            mid = pl.ds(at, BLOCK)
            applied = twice_operator(source, at)
            for field in range(3):
                target[field, mid] = (factor * base[field, mid] + target[field, mid]) - applied[field]

        for_blocks(margin, body)

    def exponential(base, direction, margin, store, last_margin):
        top = series[direction, DEG]
        for field in range(3):
            even[field] = top * base[field]
            odd[field] = jnp.zeros((span, SUBLANES, LANES), jnp.float32)

        def two_steps(j, carry):
            clenshaw(odd, even, base, series[direction, DEG - 1 - 2 * j], margin)
            clenshaw(even, odd, base, series[direction, DEG - 2 - 2 * j], margin)
            return carry

        lax.fori_loop(0, DEG // 2 - 1, two_steps, 0)
        clenshaw(odd, even, base, series[direction, 1], margin)
        factor = series[direction, 0]

        def body(at):
            mid = pl.ds(at, BLOCK)
            applied = twice_operator(odd, at)
            for field in range(3):
                store(field, at, (factor * base[field, mid] + even[field, mid]) - 0.5 * applied[field])

        for_blocks(last_margin, body)

    def advect(at):
        mid, wide = pl.ds(at, BLOCK), pl.ds(at - 1, BLOCK + 2)
        height, east, north = waves[0, wide], waves[1, wide], waves[2, wide]
        flux = height * north
        mid_east, mid_north = 0.5 * east[1:-1], 0.5 * north[1:-1]
        pulled[0, mid] = -0.5 * (lon_diff(height[1:-1] * east[1:-1]) + (flux[2:] - flux[:-2]))
        pulled[1, mid] = -(mid_east * lon_diff(east[1:-1]) + mid_north * (east[2:] - east[:-2]))
        pulled[2, mid] = -(mid_east * lon_diff(north[1:-1]) + mid_north * (north[2:] - north[:-2]))

    edges_start(coef_field, 2)
    each_peer(lambda step: gather_copy(0, step, True).start())

    for which in range(2):
        each_peer(lambda step: gather_copy(which, step, False).wait())
        tile = window.at[which]
        for field in range(3):
            tile[field, HALO : HALO + rows] = gathered[which, field]
        edges_start(tile, which)
        if which == 0:
            edges_wait(coef_field, 2)
        edges_wait(tile, which)

        def keep_wave(field, at, value):
            waves[field, pl.ds(at, BLOCK)] = value

        def keep_partial(field, at, value):
            partial[which, field, pl.ds(at - HALO, BLOCK)] = value

        exponential(tile, 0, 2 * DEG, keep_wave, 2 * DEG)
        for_blocks(DEG, advect)
        exponential(pulled, 1, DEG, keep_partial, 0)

        each_peer(lambda step: sum_copy(which, step).start())
        total = partial[which, :, pl.ds(me * share, share)]
        each_peer(lambda step: sum_copy(which, step).wait())
        for step in range(1, phases):
            total = total + parts[which, step]
        if which == 0:
            first[...] = total
            gathered[1, :, pl.ds(me * share, share)] = own[...] + time_step * total
            each_peer(lambda step: gather_copy(1, step, True).start())
        else:
            first[...] = 0.5 * (first[...] + total)

    for s in range(SUBLANES):
        lanes = pl.ds(s * LANES, LANES)
        for field in range(3):
            piece = first[field, :, s, :]
            if field == 0:
                piece = piece * radius_scale
            tend_out[field, :, lanes] = piece
            next_out[field, :, lanes] = state[field, :, lanes] + time_step * piece


def per_device(phases, lats, state_now, ocean_depth, coriolis, phase_times, phase_weights):
    rows, share = ocean_depth.shape[0], state_now.shape[1]
    span = rows + 2 * HALO
    tile = (SUBLANES, LANES)
    vmem = pl.BlockSpec(memory_space=pltpu.VMEM)
    smem = pl.BlockSpec(memory_space=pltpu.SMEM)
    out = jax.ShapeDtypeStruct(state_now.shape, jnp.float32)

    def scratch(*shape):
        return pltpu.VMEM(shape + tile, jnp.float32)

    return pl.pallas_call(
        functools.partial(kernel, phases, lats),
        out_shape=(out, out),
        in_specs=[vmem, vmem, smem, smem, smem],
        out_specs=(vmem, vmem),
        scratch_shapes=[
            scratch(3, share),
            scratch(2, 3, rows),
            scratch(2, 3, span),
            scratch(2, span),
            scratch(3, span),
            scratch(3, span),
            scratch(3, span),
            scratch(3, span),
            scratch(2, 3, rows),
            scratch(2, phases, 3, share),
            scratch(3, share),
            scratch(2, DEG + 1),
            pltpu.SemaphoreType.DMA((2, phases)),
            pltpu.SemaphoreType.DMA((2, phases)),
            pltpu.SemaphoreType.DMA((2, phases)),
            pltpu.SemaphoreType.DMA((2, phases)),
            pltpu.SemaphoreType.DMA((3, 2)),
            pltpu.SemaphoreType.DMA((3, 2)),
        ],
        compiler_params=pltpu.CompilerParams(collective_id=0, has_side_effects=True),
    )(state_now, ocean_depth, coriolis, phase_times, phase_weights)


def solution(mesh):
    placed = (P(None, ("lat", "phase"), None), P("lat", None), P("lat"), P("phase"), P("phase"))
    return jax.shard_map(
        functools.partial(per_device, mesh.shape["phase"], mesh.shape["lat"]),
        mesh=mesh,
        in_specs=placed,
        out_specs=(P(None, ("lat", "phase"), None), P(None, ("lat", "phase"), None)),
        check_vma=False,
    )
```

```python
import functools
import math

import jax
import jax.numpy as jnp
from jax import lax
from jax.experimental import pallas as pl
from jax.experimental.pallas import tpu as pltpu
from jax.sharding import PartitionSpec as P

DEG = 8
HALO = 2 * DEG + 1
BLOCK = 8
LANES = 128
SUBLANES = 8

radius_scale = 2.5
time_step = 0.5
series_terms = 20

HEIGHT_SCALE = 1.0 / radius_scale
DEPTH_SCALE = 1.0 / (radius_scale * radius_scale)
ROTATION_SCALE = 2.0 / radius_scale


def slabs_of(phases):
    return 4 if phases % 4 == 0 else 1


def partner(index, step, count):
    if count == 4:
        return [index, index + 1 - 2 * lax.rem(index, 2), lax.rem(index + 2, 4), 3 - index][step]
    return lax.rem(index + step, count)


def source_of(index, step, count):
    if count == 4:
        return partner(index, step, count)
    return lax.rem(index + count - step, count)


def kernel(
    phases,
    lats,
    state,
    depth,
    coriolis,
    times,
    weights,
    next_out,
    tend_out,
    own,
    gathered,
    window,
    coef_field,
    even,
    odd,
    waves,
    pulled,
    partial,
    parts,
    staged,
    first,
    series,
    outer_send,
    outer_recv,
    inner_send,
    inner_recv,
    halo_send,
    halo_recv,
):
    rows, share = depth.shape[0], state.shape[1]
    me, lat = lax.axis_index("phase"), lax.axis_index("lat")
    outer = slabs_of(phases)
    inner = phases // outer
    slab, place = me // inner, lax.rem(me, inner)
    below = (lat + lats - 1) // lats
    above = (2 * lats - 2 - lat) // lats
    span = window.shape[2]

    zero = jnp.zeros((HALO, SUBLANES, LANES), jnp.float32)
    for array in (window.at[0], window.at[1]):
        for field in range(3):
            array[field, 0:HALO] = zero
            array[field, HALO + rows : span] = zero
    for field in range(2):
        coef_field[field, 0:HALO] = zero
        coef_field[field, HALO + rows : span] = zero

    barrier = pltpu.get_barrier_semaphore()

    for step in range(1, outer):
        pl.semaphore_signal(barrier, inc=1, device_id={"phase": partner(slab, step, outer) * inner + place})
    for step in range(1, inner):
        pl.semaphore_signal(barrier, inc=1, device_id={"phase": slab * inner + partner(place, step, inner)})

    @pl.when(lat > 0)
    def _():
        pl.semaphore_signal(barrier, inc=1, device_id={"lat": lat - 1})

    @pl.when(lat < lats - 1)
    def _():
        pl.semaphore_signal(barrier, inc=1, device_id={"lat": lat + 1})

    for s in range(SUBLANES):
        lanes = pl.ds(s * LANES, LANES)
        for field in range(3):
            piece = state[field, :, lanes]
            own[field, :, s, :] = piece * HEIGHT_SCALE if field == 0 else piece
        coef_field[0, HALO : HALO + rows, s, :] = depth[:, lanes] * DEPTH_SCALE
    for row in range(rows):
        coef_field[1, HALO + row] = jnp.full((SUBLANES, LANES), coriolis[row] * ROTATION_SCALE, jnp.float32)
    gathered[0, :, pl.ds(me * share, share)] = own[...]

    half_time = jnp.full((SUBLANES, LANES), times[0] * 0.5, jnp.float32)
    weight = jnp.full((SUBLANES, LANES), weights[0], jnp.float32)
    square = half_time * half_time
    power = jnp.ones_like(half_time)
    for degree in range(DEG + 1):
        summed = jnp.zeros_like(square)
        for term in reversed(range(series_terms)):
            factor = (-1.0) ** term / (math.factorial(term) * math.factorial(term + degree))
            summed = summed * square + factor
        value = summed * power
        if degree > 0:
            value = 2.0 * value
        series[0, degree] = value
        series[1, degree] = weight * (value if degree % 2 == 0 else -value)
        power = power * half_time

    zero = jnp.zeros((span, SUBLANES, LANES), jnp.float32)
    for field in range(3):
        waves[field] = zero
        pulled[field] = zero

    pl.semaphore_wait(barrier, outer - 1 + inner - 1 + below + above)

    def chunk(group, at):
        return pl.ds((group * inner + at) * share, share)

    def outer_gather(which, step):
        at = chunk(slab, place)
        return pltpu.make_async_remote_copy(
            src_ref=gathered.at[which, :, at],
            dst_ref=gathered.at[which, :, at],
            send_sem=outer_send.at[which, step],
            recv_sem=outer_recv.at[which, step],
            device_id={"phase": partner(slab, step, outer) * inner + place},
        )

    def inner_gather(which, held, step):
        at = chunk(source_of(slab, held, outer), place)
        return pltpu.make_async_remote_copy(
            src_ref=gathered.at[which, :, at],
            dst_ref=gathered.at[which, :, at],
            send_sem=inner_send.at[which, held, step],
            recv_sem=inner_recv.at[which, held, step],
            device_id={"phase": slab * inner + partner(place, step, inner)},
        )

    def inner_sum(which, held, step):
        peer = partner(place, step, inner)
        return pltpu.make_async_remote_copy(
            src_ref=partial.at[which, :, chunk(partner(slab, held, outer), peer)],
            dst_ref=parts.at[which, held, step],
            send_sem=inner_send.at[2 + which, held, step],
            recv_sem=inner_recv.at[2 + which, held, step],
            device_id={"phase": slab * inner + peer},
        )

    def outer_sum(which, step):
        return pltpu.make_async_remote_copy(
            src_ref=staged.at[which, step],
            dst_ref=parts.at[which, step, 0],
            send_sem=outer_send.at[2 + which, step],
            recv_sem=outer_recv.at[2 + which, step],
            device_id={"phase": partner(slab, step, outer) * inner + place},
        )

    def gather_start(which):
        for step in range(1, outer):
            outer_gather(which, step).start()
        for step in range(1, inner):
            inner_gather(which, 0, step).start()

    def gather_finish(which):
        for held in range(1, outer):
            outer_gather(which, held).wait_recv()
            for step in range(1, inner):
                inner_gather(which, held, step).start()
        for step in range(1, outer):
            outer_gather(which, step).wait_send()
        for held in range(outer):
            for step in range(1, inner):
                inner_gather(which, held, step).wait()

    def sum_over_phase(which):
        order = list(reversed(range(outer)))
        for held in order:
            for step in range(1, inner):
                inner_sum(which, held, step).start()
        for held in order:
            total = partial[which, :, chunk(partner(slab, held, outer), place)]
            for step in range(1, inner):
                inner_sum(which, held, step).wait()
                total = total + parts[which, held, step]
            if held > 0:
                staged[which, held] = total
                outer_sum(which, held).start()
        for step in range(1, outer):
            outer_sum(which, step).wait()
            total = total + parts[which, step, 0]
        return total

    def edge_copies(array, index):
        up = pltpu.make_async_remote_copy(
            src_ref=array.at[:, pl.ds(rows, HALO)],
            dst_ref=array.at[:, pl.ds(0, HALO)],
            send_sem=halo_send.at[index, 0],
            recv_sem=halo_recv.at[index, 0],
            device_id={"lat": lat + 1},
        )
        down = pltpu.make_async_remote_copy(
            src_ref=array.at[:, pl.ds(HALO, HALO)],
            dst_ref=array.at[:, pl.ds(HALO + rows, HALO)],
            send_sem=halo_send.at[index, 1],
            recv_sem=halo_recv.at[index, 1],
            device_id={"lat": lat - 1},
        )
        return up, down

    def edges_start(array, index):
        up, down = edge_copies(array, index)
        pl.when(lat < lats - 1)(up.start)
        pl.when(lat > 0)(down.start)

    def edges_wait(array, index):
        up, down = edge_copies(array, index)

        @pl.when(lat < lats - 1)
        def _():
            up.wait_send()
            down.wait_recv()

        @pl.when(lat > 0)
        def _():
            down.wait_send()
            up.wait_recv()

    lane = lax.broadcasted_iota(jnp.int32, (BLOCK, SUBLANES, LANES), 2)
    last_lane, first_lane = lane == LANES - 1, lane == 0

    def lon_diff(values):
        after = pltpu.roll(values, LANES - 1, 2)
        after = jnp.where(last_lane, pltpu.roll(after, SUBLANES - 1, 1), after)
        before = pltpu.roll(values, 1, 2)
        before = jnp.where(first_lane, pltpu.roll(before, 1, 1), before)
        return after - before

    def for_blocks(margin, fn):
        start = HALO - margin * below

        def body(i, carry):
            fn(start + i * BLOCK)
            return carry

        if lats == 2:
            lax.fori_loop(0, (rows + margin) // BLOCK, body, 0, unroll=True)
        else:
            lax.fori_loop(0, (rows + margin * (below + above)) // BLOCK, body, 0)

    def twice_operator(source, at):
        mid, wide = pl.ds(at, BLOCK), pl.ds(at - 1, BLOCK + 2)
        height = source[0, wide]
        east = source[1, mid]
        north = source[2, wide]
        flux = coef_field[0, wide] * north
        rotation = coef_field[1, mid]
        height_part = lon_diff(coef_field[0, mid] * east) + (flux[2:] - flux[:-2])
        east_part = lon_diff(height[1:-1]) - rotation * north[1:-1]
        north_part = (height[2:] - height[:-2]) + rotation * east
        return height_part, east_part, north_part

    def clenshaw(target, source, base, factor, margin):
        def body(at):
            mid = pl.ds(at, BLOCK)
            applied = twice_operator(source, at)
            for field in range(3):
                target[field, mid] = (factor * base[field, mid] + target[field, mid]) - applied[field]

        for_blocks(margin, body)

    def exponential(base, direction, margin, store, last_margin):
        top = series[direction, DEG]
        for field in range(3):
            even[field] = top * base[field]
            odd[field] = jnp.zeros((span, SUBLANES, LANES), jnp.float32)

        def two_steps(j, carry):
            clenshaw(odd, even, base, series[direction, DEG - 1 - 2 * j], margin)
            clenshaw(even, odd, base, series[direction, DEG - 2 - 2 * j], margin)
            return carry

        lax.fori_loop(0, DEG // 2 - 1, two_steps, 0)
        clenshaw(odd, even, base, series[direction, 1], margin)
        factor = series[direction, 0]

        def body(at):
            mid = pl.ds(at, BLOCK)
            applied = twice_operator(odd, at)
            for field in range(3):
                store(field, at, (factor * base[field, mid] + even[field, mid]) - 0.5 * applied[field])

        for_blocks(last_margin, body)

    def advect(at):
        mid, wide = pl.ds(at, BLOCK), pl.ds(at - 1, BLOCK + 2)
        height, east, north = waves[0, wide], waves[1, wide], waves[2, wide]
        flux = height * north
        mid_east, mid_north = 0.5 * east[1:-1], 0.5 * north[1:-1]
        pulled[0, mid] = -0.5 * (lon_diff(height[1:-1] * east[1:-1]) + (flux[2:] - flux[:-2]))
        pulled[1, mid] = -(mid_east * lon_diff(east[1:-1]) + mid_north * (east[2:] - east[:-2]))
        pulled[2, mid] = -(mid_east * lon_diff(north[1:-1]) + mid_north * (north[2:] - north[:-2]))

    edges_start(coef_field, 2)
    gather_start(0)

    for which in range(2):
        gather_finish(which)
        tile = window.at[which]
        for field in range(3):
            tile[field, HALO : HALO + rows] = gathered[which, field]
        edges_start(tile, which)
        if which == 0:
            edges_wait(coef_field, 2)
        edges_wait(tile, which)

        def keep_wave(field, at, value):
            waves[field, pl.ds(at, BLOCK)] = value

        def keep_partial(field, at, value):
            partial[which, field, pl.ds(at - HALO, BLOCK)] = value

        exponential(tile, 0, 2 * DEG, keep_wave, 2 * DEG)
        for_blocks(DEG, advect)
        exponential(pulled, 1, DEG, keep_partial, 0)

        total = sum_over_phase(which)
        if which == 0:
            first[...] = total
            gathered[1, :, pl.ds(me * share, share)] = own[...] + time_step * total
            gather_start(1)
        else:
            first[...] = 0.5 * (first[...] + total)

    for s in range(SUBLANES):
        lanes = pl.ds(s * LANES, LANES)
        for field in range(3):
            piece = first[field, :, s, :]
            if field == 0:
                piece = piece * radius_scale
            tend_out[field, :, lanes] = piece
            next_out[field, :, lanes] = state[field, :, lanes] + time_step * piece


def per_device(phases, lats, state_now, ocean_depth, coriolis, phase_times, phase_weights):
    rows, share = ocean_depth.shape[0], state_now.shape[1]
    span = rows + 2 * HALO
    outer = slabs_of(phases)
    inner = phases // outer
    tile = (SUBLANES, LANES)
    vmem = pl.BlockSpec(memory_space=pltpu.VMEM)
    smem = pl.BlockSpec(memory_space=pltpu.SMEM)
    out = jax.ShapeDtypeStruct(state_now.shape, jnp.float32)

    def scratch(*shape):
        return pltpu.VMEM(shape + tile, jnp.float32)

    return pl.pallas_call(
        functools.partial(kernel, phases, lats),
        out_shape=(out, out),
        in_specs=[vmem, vmem, smem, smem, smem],
        out_specs=(vmem, vmem),
        scratch_shapes=[
            scratch(3, share),
            scratch(2, 3, rows),
            scratch(2, 3, span),
            scratch(2, span),
            scratch(3, span),
            scratch(3, span),
            scratch(3, span),
            scratch(3, span),
            scratch(2, 3, rows),
            scratch(2, outer, inner, 3, share),
            scratch(2, outer, 3, share),
            scratch(3, share),
            scratch(2, DEG + 1),
            pltpu.SemaphoreType.DMA((4, outer)),
            pltpu.SemaphoreType.DMA((4, outer)),
            pltpu.SemaphoreType.DMA((4, outer, inner)),
            pltpu.SemaphoreType.DMA((4, outer, inner)),
            pltpu.SemaphoreType.DMA((3, 2)),
            pltpu.SemaphoreType.DMA((3, 2)),
        ],
        compiler_params=pltpu.CompilerParams(collective_id=0, has_side_effects=True),
    )(state_now, ocean_depth, coriolis, phase_times, phase_weights)


def solution(mesh):
    placed = (P(None, ("lat", "phase"), None), P("lat", None), P("lat"), P("phase"), P("phase"))
    return jax.shard_map(
        functools.partial(per_device, mesh.shape["phase"], mesh.shape["lat"]),
        mesh=mesh,
        in_specs=placed,
        out_specs=(P(None, ("lat", "phase"), None), P(None, ("lat", "phase"), None)),
        check_vma=False,
    )
```

```python
import functools
import math

import jax
import jax.numpy as jnp
from jax import lax
from jax.experimental import pallas as pl
from jax.experimental.pallas import tpu as pltpu
from jax.sharding import PartitionSpec as P

DEG = 8
HALO = 2 * DEG + 1
BLOCK = 8
LANES = 128
SUBLANES = 8

radius_scale = 2.5
time_step = 0.5
series_terms = 20

HEIGHT_SCALE = 1.0 / radius_scale
DEPTH_SCALE = 1.0 / (radius_scale * radius_scale)
ROTATION_SCALE = 2.0 / radius_scale


def slabs_of(phases):
    return 4 if phases % 4 == 0 else 1


def partner(index, step, count):
    if count == 4:
        return [index, index + 1 - 2 * lax.rem(index, 2), lax.rem(index + 2, 4), 3 - index][step]
    return lax.rem(index + step, count)


def source_of(index, step, count):
    if count == 4:
        return partner(index, step, count)
    return lax.rem(index + count - step, count)


def kernel(
    phases,
    lats,
    state_in,
    depth_in,
    coriolis,
    times,
    weights,
    tend_out,
    state,
    depth,
    own,
    gathered,
    window,
    coef_field,
    even,
    odd,
    waves,
    pulled,
    partial,
    parts,
    staged,
    first,
    series,
    outer_send,
    outer_recv,
    inner_send,
    inner_recv,
    halo_send,
    halo_recv,
    input_sem,
):
    rows, share = depth.shape[0], state.shape[1]
    me, lat = lax.axis_index("phase"), lax.axis_index("lat")
    outer = slabs_of(phases)
    inner = phases // outer
    slab, place = me // inner, lax.rem(me, inner)
    below = (lat + lats - 1) // lats
    above = (2 * lats - 2 - lat) // lats
    span = window.shape[2]

    copies = [
        pltpu.make_async_copy(state_in, state, input_sem.at[0]),
        pltpu.make_async_copy(depth_in, depth, input_sem.at[1]),
    ]
    for copy in copies:
        copy.start()
    barrier = pltpu.get_barrier_semaphore()

    for step in range(1, outer):
        pl.semaphore_signal(barrier, inc=1, device_id={"phase": partner(slab, step, outer) * inner + place})
    for step in range(1, inner):
        pl.semaphore_signal(barrier, inc=1, device_id={"phase": slab * inner + partner(place, step, inner)})

    zero = jnp.zeros((HALO, SUBLANES, LANES), jnp.float32)
    for array in (window.at[0], window.at[1]):
        for field in range(3):
            array[field, 0:HALO] = zero
            array[field, HALO + rows : span] = zero
    for field in range(2):
        coef_field[field, 0:HALO] = zero
        coef_field[field, HALO + rows : span] = zero

    @pl.when(lat > 0)
    def _():
        pl.semaphore_signal(barrier, inc=1, device_id={"lat": lat - 1})

    @pl.when(lat < lats - 1)
    def _():
        pl.semaphore_signal(barrier, inc=1, device_id={"lat": lat + 1})

    copies[0].wait()
    for s in range(SUBLANES):
        for field in range(3):
            piece = state[field, :, s * LANES : (s + 1) * LANES]
            own[field, :, s, :] = piece * HEIGHT_SCALE if field == 0 else piece
    gathered[0, :, pl.ds(me * share, share)] = own[...]

    pl.semaphore_wait(barrier, outer - 1 + inner - 1 + below + above)

    def chunk(group, at):
        return pl.ds((group * inner + at) * share, share)

    def outer_gather(which, step):
        at = chunk(slab, place)
        return pltpu.make_async_remote_copy(
            src_ref=gathered.at[which, :, at],
            dst_ref=gathered.at[which, :, at],
            send_sem=outer_send.at[which, step],
            recv_sem=outer_recv.at[which, step],
            device_id={"phase": partner(slab, step, outer) * inner + place},
        )

    def inner_gather(which, held, step):
        at = chunk(source_of(slab, held, outer), place)
        return pltpu.make_async_remote_copy(
            src_ref=gathered.at[which, :, at],
            dst_ref=gathered.at[which, :, at],
            send_sem=inner_send.at[which, held, step],
            recv_sem=inner_recv.at[which, held, step],
            device_id={"phase": slab * inner + partner(place, step, inner)},
        )

    def inner_sum(which, held, step):
        peer = partner(place, step, inner)
        return pltpu.make_async_remote_copy(
            src_ref=partial.at[which, :, chunk(partner(slab, held, outer), peer)],
            dst_ref=parts.at[which, held, step],
            send_sem=inner_send.at[2 + which, held, step],
            recv_sem=inner_recv.at[2 + which, held, step],
            device_id={"phase": slab * inner + peer},
        )

    def outer_sum(which, step):
        return pltpu.make_async_remote_copy(
            src_ref=staged.at[which, step],
            dst_ref=parts.at[which, step, 0],
            send_sem=outer_send.at[2 + which, step],
            recv_sem=outer_recv.at[2 + which, step],
            device_id={"phase": partner(slab, step, outer) * inner + place},
        )

    def gather_start(which):
        for step in range(1, outer):
            outer_gather(which, step).start()
        for step in range(1, inner):
            inner_gather(which, 0, step).start()

    def gather_finish(which):
        for held in range(1, outer):
            outer_gather(which, held).wait_recv()
            for step in range(1, inner):
                inner_gather(which, held, step).start()
        for step in range(1, outer):
            outer_gather(which, step).wait_send()
        for held in range(outer):
            for step in range(1, inner):
                inner_gather(which, held, step).wait()

    def sum_over_phase(which):
        order = list(reversed(range(outer)))
        for held in order:
            for step in range(1, inner):
                inner_sum(which, held, step).start()
        for held in order:
            total = partial[which, :, chunk(partner(slab, held, outer), place)]
            for step in range(1, inner):
                inner_sum(which, held, step).wait()
                total = total + parts[which, held, step]
            if held > 0:
                staged[which, held] = total
                outer_sum(which, held).start()
        for step in range(1, outer):
            outer_sum(which, step).wait()
            total = total + parts[which, step, 0]
        return total

    def edge_copies(array, index):
        up = pltpu.make_async_remote_copy(
            src_ref=array.at[:, pl.ds(rows, HALO)],
            dst_ref=array.at[:, pl.ds(0, HALO)],
            send_sem=halo_send.at[index, 0],
            recv_sem=halo_recv.at[index, 0],
            device_id={"lat": lat + 1},
        )
        down = pltpu.make_async_remote_copy(
            src_ref=array.at[:, pl.ds(HALO, HALO)],
            dst_ref=array.at[:, pl.ds(HALO + rows, HALO)],
            send_sem=halo_send.at[index, 1],
            recv_sem=halo_recv.at[index, 1],
            device_id={"lat": lat - 1},
        )
        return up, down

    def edges_start(array, index):
        up, down = edge_copies(array, index)
        pl.when(lat < lats - 1)(up.start)
        pl.when(lat > 0)(down.start)

    def edges_wait(array, index):
        up, down = edge_copies(array, index)

        @pl.when(lat < lats - 1)
        def _():
            up.wait_send()
            down.wait_recv()

        @pl.when(lat > 0)
        def _():
            down.wait_send()
            up.wait_recv()

    lane = lax.broadcasted_iota(jnp.int32, (BLOCK, SUBLANES, LANES), 2)
    last_lane, first_lane = lane == LANES - 1, lane == 0

    def lon_diff(values):
        after = pltpu.roll(values, LANES - 1, 2)
        after = jnp.where(last_lane, pltpu.roll(after, SUBLANES - 1, 1), after)
        before = pltpu.roll(values, 1, 2)
        before = jnp.where(first_lane, pltpu.roll(before, 1, 1), before)
        return after - before

    def for_blocks(margin, fn):
        start = HALO - margin * below

        def body(i, carry):
            fn(start + i * BLOCK)
            return carry

        if lats == 2:
            lax.fori_loop(0, (rows + margin) // BLOCK, body, 0, unroll=True)
        else:
            lax.fori_loop(0, (rows + margin * (below + above)) // BLOCK, body, 0)

    def twice_operator(source, at):
        mid, wide = pl.ds(at, BLOCK), pl.ds(at - 1, BLOCK + 2)
        height = source[0, wide]
        east = source[1, mid]
        north = source[2, wide]
        flux = coef_field[0, wide] * north
        rotation = coef_field[1, mid]
        height_part = lon_diff(coef_field[0, mid] * east) + (flux[2:] - flux[:-2])
        east_part = lon_diff(height[1:-1]) - rotation * north[1:-1]
        north_part = (height[2:] - height[:-2]) + rotation * east
        return height_part, east_part, north_part

    def clenshaw(target, source, base, factor, margin):
        def body(at):
            mid = pl.ds(at, BLOCK)
            applied = twice_operator(source, at)
            for field in range(3):
                target[field, mid] = (factor * base[field, mid] + target[field, mid]) - applied[field]

        for_blocks(margin, body)

    def fill(base, direction, start, count):
        at = pl.ds(start, count)
        top = series[direction, DEG]
        for field in range(3):
            even[field, at] = top * base[field, at]
            odd[field, at] = jnp.zeros((count, SUBLANES, LANES), jnp.float32)

    def exponential(base, direction, margin, store, last_margin):
        def two_steps(j, carry):
            clenshaw(odd, even, base, series[direction, DEG - 1 - 2 * j], margin)
            clenshaw(even, odd, base, series[direction, DEG - 2 - 2 * j], margin)
            return carry

        lax.fori_loop(0, DEG // 2 - 1, two_steps, 0)
        clenshaw(odd, even, base, series[direction, 1], margin)
        factor = series[direction, 0]

        def body(at):
            mid = pl.ds(at, BLOCK)
            applied = twice_operator(odd, at)
            for field in range(3):
                store(field, at, (factor * base[field, mid] + even[field, mid]) - 0.5 * applied[field])

        for_blocks(last_margin, body)

    def advect(at):
        mid, wide = pl.ds(at, BLOCK), pl.ds(at - 1, BLOCK + 2)
        height, east, north = waves[0, wide], waves[1, wide], waves[2, wide]
        flux = height * north
        mid_east, mid_north = 0.5 * east[1:-1], 0.5 * north[1:-1]
        pulled[0, mid] = -0.5 * (lon_diff(height[1:-1] * east[1:-1]) + (flux[2:] - flux[:-2]))
        pulled[1, mid] = -(mid_east * lon_diff(east[1:-1]) + mid_north * (east[2:] - east[:-2]))
        pulled[2, mid] = -(mid_east * lon_diff(north[1:-1]) + mid_north * (north[2:] - north[:-2]))

    gather_start(0)

    copies[1].wait()
    for s in range(SUBLANES):
        coef_field[0, HALO : HALO + rows, s, :] = depth[:, s * LANES : (s + 1) * LANES] * DEPTH_SCALE
    for row in range(rows):
        coef_field[1, HALO + row] = jnp.full((SUBLANES, LANES), coriolis[row] * ROTATION_SCALE, jnp.float32)
    edges_start(coef_field, 2)

    half_time = jnp.full((SUBLANES, LANES), times[0] * 0.5, jnp.float32)
    weight = jnp.full((SUBLANES, LANES), weights[0], jnp.float32)
    square = half_time * half_time
    power = jnp.ones_like(half_time)
    for degree in range(DEG + 1):
        summed = jnp.zeros_like(square)
        for term in reversed(range(series_terms)):
            factor = (-1.0) ** term / (math.factorial(term) * math.factorial(term + degree))
            summed = summed * square + factor
        value = summed * power
        if degree > 0:
            value = 2.0 * value
        series[0, degree] = value
        series[1, degree] = weight * (value if degree % 2 == 0 else -value)
        power = power * half_time

    zero = jnp.zeros((span, SUBLANES, LANES), jnp.float32)
    for field in range(3):
        waves[field] = zero
        pulled[field] = zero


    for which in range(2):
        gather_finish(which)
        tile = window.at[which]
        for field in range(3):
            tile[field, HALO : HALO + rows] = gathered[which, field]
        edges_start(tile, which)
        fill(tile, 0, HALO, rows)
        if which == 0:
            edges_wait(coef_field, 2)
        edges_wait(tile, which)
        fill(tile, 0, 0, HALO)
        fill(tile, 0, HALO + rows, HALO)

        def keep_wave(field, at, value):
            waves[field, pl.ds(at, BLOCK)] = value

        def keep_partial(field, at, value):
            partial[which, field, pl.ds(at - HALO, BLOCK)] = value

        exponential(tile, 0, 2 * DEG, keep_wave, 2 * DEG)
        for_blocks(DEG, advect)
        fill(pulled, 1, 0, span)
        exponential(pulled, 1, DEG, keep_partial, 0)

        total = sum_over_phase(which)
        if which == 0:
            first[...] = total
            gathered[1, :, pl.ds(me * share, share)] = own[...] + time_step * total
            gather_start(1)
        else:
            first[...] = 0.5 * (first[...] + total)

    for s in range(SUBLANES):
        lanes = pl.ds(s * LANES, LANES)
        for field in range(3):
            piece = first[field, :, s, :]
            if field == 0:
                piece = piece * radius_scale
            tend_out[field, :, lanes] = piece


def finish(state, tendency, next_out, tend_out):
    tend_out[...] = tendency[...]
    next_out[...] = state[...] + time_step * tendency[...]


def per_device(phases, lats, state_now, ocean_depth, coriolis, phase_times, phase_weights):
    rows, share = ocean_depth.shape[0], state_now.shape[1]
    span = rows + 2 * HALO
    outer = slabs_of(phases)
    inner = phases // outer
    tile = (SUBLANES, LANES)
    vmem = pl.BlockSpec(memory_space=pltpu.VMEM)
    smem = pl.BlockSpec(memory_space=pltpu.SMEM)
    out = jax.ShapeDtypeStruct(state_now.shape, jnp.float32)

    def scratch(*shape):
        return pltpu.VMEM(shape + tile, jnp.float32)

    any_space = pl.BlockSpec(memory_space=pl.ANY)
    tendency = pl.pallas_call(
        functools.partial(kernel, phases, lats),
        out_shape=out,
        in_specs=[any_space, any_space, smem, smem, smem],
        out_specs=vmem,
        scratch_shapes=[
            pltpu.VMEM(state_now.shape, jnp.float32),
            pltpu.VMEM(ocean_depth.shape, jnp.float32),
            scratch(3, share),
            scratch(2, 3, rows),
            scratch(2, 3, span),
            scratch(2, span),
            scratch(3, span),
            scratch(3, span),
            scratch(3, span),
            scratch(3, span),
            scratch(2, 3, rows),
            scratch(2, outer, inner, 3, share),
            scratch(2, outer, 3, share),
            scratch(3, share),
            scratch(2, DEG + 1),
            pltpu.SemaphoreType.DMA((4, outer)),
            pltpu.SemaphoreType.DMA((4, outer)),
            pltpu.SemaphoreType.DMA((4, outer, inner)),
            pltpu.SemaphoreType.DMA((4, outer, inner)),
            pltpu.SemaphoreType.DMA((3, 2)),
            pltpu.SemaphoreType.DMA((3, 2)),
            pltpu.SemaphoreType.DMA((2,)),
        ],
        compiler_params=pltpu.CompilerParams(collective_id=0, has_side_effects=True),
    )(state_now, ocean_depth, coriolis, phase_times, phase_weights)
    return pl.pallas_call(
        finish,
        out_shape=(out, out),
        in_specs=[vmem, vmem],
        out_specs=(vmem, vmem),
    )(state_now, tendency)


def solution(mesh):
    placed = (P(None, ("lat", "phase"), None), P("lat", None), P("lat"), P("phase"), P("phase"))
    return jax.shard_map(
        functools.partial(per_device, mesh.shape["phase"], mesh.shape["lat"]),
        mesh=mesh,
        in_specs=placed,
        out_specs=(P(None, ("lat", "phase"), None), P(None, ("lat", "phase"), None)),
        check_vma=False,
    )
```
